32 devices in a mesh: gx: 4 (over z), gy: 8 (over y, x, core).
Axes of the slice: x: 2, y: 2, z: 4, core: 2. Of those that a mesh axis runs over, the one named last changes fastest.
Arguments:
- right_side: float32 [2048, 4096], P('gx', 'gy'), may hold values from -8 to 8
- drift_x: float32 [2048, 4096], P('gx', 'gy'), may hold values from -0.9 to 0.9
- drift_y: float32 [2048, 4096], P('gx', 'gy'), may hold values from -0.9 to 0.9
- sketch_rows: float32 [256, 2048], P(None, 'gx'), may hold values from -0.375 to 0.375
- sketch_cols: float32 [256, 4096], P(None, 'gy'), may hold values from -6 to 6
Outputs:
- solution: float32 [2048, 4096], P('gx', 'gy')
- residual: float32 [2048, 4096], P('gx', 'gy')
The draws below stay inside these ranges and needn't reach their ends.
All inputs are finite; a program needn't handle non-finite values.
Results may differ from the reference program's by a relative error of at most 0.0003.
Values sent between devices are 32-bit elements; how exact they have to be, the bound alone decides.
A program may use at most 64 MiB of HBM per device.

```python
import jax
import jax.numpy as jnp
from jax import lax

K = 256
ITERS = 4
NX = 2048
NY = 4096


def block_scale(stream_key, shape, pieces, smallest, largest):
    loudness, own = 1.0, jax.random.fold_in(stream_key, 6)
    for axis_at, parts in pieces:
        draws = jnp.exp(jax.random.uniform(jax.random.fold_in(own, axis_at), (parts,), jnp.float32, smallest / len(pieces), largest / len(pieces)))
        loudness = loudness * jnp.repeat(draws, shape[axis_at] // parts).reshape([-1 if axis == axis_at else 1 for axis in range(len(shape))])
    return loudness


def noise(key, shape, scale, most, shards=(), kind=jnp.bfloat16):
    level = block_scale(key, shape, shards, -0.22, 0.18) if shards else 1.0
    values = jax.random.normal(key, shape, jnp.float32) * scale * level
    return jnp.minimum(jnp.maximum(values, -most), most).astype(kind)


def setup_inputs(seed: int = 0) -> dict:
    keys = jax.random.split(jax.random.key(seed), 6)
    right_side = noise(keys[0], (NX, NY), 1.0, 8.0, ((0, 4), (1, 8)), jnp.float32)
    drift_x = jnp.clip(jax.random.uniform(keys[1], (NX, NY), jnp.float32, -0.9, 0.9) * block_scale(keys[1], (NX, NY), ((0, 4), (1, 8)), -0.4, 0.0), -0.9, 0.9)
    drift_y = jnp.clip(jax.random.uniform(keys[2], (NX, NY), jnp.float32, -0.9, 0.9) * block_scale(keys[2], (NX, NY), ((0, 4), (1, 8)), -0.4, 0.0), -0.9, 0.9)
    sketch_rows = noise(keys[3], (K, NX), K ** -0.5, 0.375, ((1, 4),), jnp.float32)
    sketch_cols = noise(keys[4], (K, NY), 1.0, 6.0, ((1, 8),), jnp.float32)
    return dict(right_side=right_side, drift_x=drift_x, drift_y=drift_y, sketch_rows=sketch_rows, sketch_cols=sketch_cols)


shift_value = 0.05

def operate(field, drift_x, drift_y):
    padded = jnp.pad(field, 1)
    upper_cells = padded[:-2, 1:-1]
    lower_cells = padded[2:, 1:-1]
    left_cells = padded[1:-1, :-2]
    right_cells = padded[1:-1, 2:]
    return (4.0 + shift_value) * field - (1.0 + drift_x) * upper_cells - (1.0 - drift_x) * lower_cells - (1.0 + drift_y) * left_cells - (1.0 - drift_y) * right_cells

def sketch(field, sketch_rows, sketch_cols):
    product = jnp.dot(field, sketch_cols.T, precision=lax.Precision.HIGHEST)
    return jnp.einsum('ki,ik->k', sketch_rows, product, precision=lax.Precision.HIGHEST)

def solve_small(hessenberg, beta_norm):
    gram_matrix = jnp.dot(hessenberg.T, hessenberg, precision=lax.Precision.HIGHEST)
    target = beta_norm * hessenberg[0]
    factor = jnp.linalg.cholesky(gram_matrix)
    count = hessenberg.shape[1]
    forward = []
    for row in range(count):
        acc = target[row]
        for col in range(row):
            acc = acc - factor[row, col] * forward[col]
        forward.append(acc / factor[row, row])
    backward = [None] * count
    for row in reversed(range(count)):
        acc = forward[row]
        for col in range(row + 1, count):
            acc = acc - factor[col, row] * backward[col]
        backward[row] = acc / factor[row, row]
    return backward

def reference(right_side, drift_x, drift_y, sketch_rows, sketch_cols):
    first_sketch = sketch(right_side, sketch_rows, sketch_cols)
    beta_norm = jnp.sqrt(jnp.sum(first_sketch * first_sketch))
    basis_vectors = [right_side / beta_norm]
    sketched = [first_sketch / beta_norm]
    columns = []
    for column in range(ITERS):
        applied = operate(basis_vectors[column], drift_x, drift_y)
        sketch_image = sketch(applied, sketch_rows, sketch_cols)
        sketch_matrix = jnp.stack(sketched, axis=1)
        projection = jnp.dot(sketch_matrix.T, sketch_image, precision=lax.Precision.HIGHEST)
        remainder = applied
        for index_prev in range(column + 1):
            remainder = remainder - projection[index_prev] * basis_vectors[index_prev]
        remainder_sketch = sketch(remainder, sketch_rows, sketch_cols)
        new_norm = jnp.sqrt(jnp.sum(remainder_sketch * remainder_sketch))
        basis_vectors.append(remainder / new_norm)
        sketched.append(remainder_sketch / new_norm)
        entries = jnp.concatenate([projection, new_norm[None], jnp.zeros((ITERS - column - 1,), jnp.float32)])
        columns.append(entries)
    hessenberg = jnp.stack(columns, axis=1)
    coeffs = solve_small(hessenberg, beta_norm)
    solution = jnp.zeros_like(right_side)
    for column in range(ITERS):
        solution = solution + coeffs[column] * basis_vectors[column]
    residual = right_side - operate(solution, drift_x, drift_y)
    return (solution, residual)
```

```python
import jax
import jax.numpy as jnp
from jax import lax
from jax.experimental import pallas as pl
from jax.experimental.pallas import tpu as pltpu
from jax.sharding import PartitionSpec as P

ITERS = 4
CENTER = 4.0 + 0.05
L = 128
PAD = 16
EDGE = 8
MESH = pl.DeviceIdType.MESH
SIDES = [(-1, 0), (1, 0), (0, -1), (0, 1), (-1, -1), (-1, 1), (1, -1), (1, 1)]


def solve_small(gram):
    n = ITERS

    def g(a, b):
        return gram[(min(a, b), max(a, b))]

    f = {}
    for a in range(n + 1):
        for j in range(n):
            value = CENTER * g(a, j) + 2.0 * g(a, j + 1)
            f[a, j] = value + 2.0 * g(a, j - 1) if j else value
    m = {}
    for i in range(n):
        for j in range(i + 1):
            value = CENTER * f[i, j] + 2.0 * f[i + 1, j]
            m[i, j] = value + 2.0 * f[i - 1, j] if i else value
    inv, low, scaled = [], {}, {}
    for j in range(n):
        for i in range(j, n):
            acc = m[i, j]
            for k in range(j):
                acc = acc - scaled[i, k] * low[j, k]
            scaled[i, j] = acc
        inv.append(1.0 / scaled[j, j])
        for i in range(j + 1, n):
            low[i, j] = scaled[i, j] * inv[j]
    forward = []
    for i in range(n):
        acc = f[0, i]
        for k in range(i):
            acc = acc - low[i, k] * forward[k]
        forward.append(acc)
    y = [None] * n
    for i in reversed(range(n)):
        acc = forward[i] * inv[i]
        for k in range(i + 1, n):
            acc = acc - low[k, i] * y[k]
        y[i] = acc
    res = []
    for k in range(n + 1):
        z = 0.0
        if k < n:
            z = z + CENTER * y[k]
        if k >= 1:
            z = z + 2.0 * y[k - 1]
        if k + 1 < n:
            z = z + 2.0 * y[k + 1]
        res.append(1.0 - z if k == 0 else -z)
    return y, res


def kernel(nx, ny, b_hbm, dx_hbm, dy_hbm, rows_hbm, cols_hbm, x_hbm, r_hbm,
           ext, basis, rows_v, cols_v, rows_t, ct_hi, ct_lo, col_out, col_in, diag_out, diag_in,
           part, got_x, sum_x, got_y, x_v, r_v,
           in_sem, out_sem, hs_sem, hr_sem, xs_sem, xr_sem, ys_sem, yr_sem):
    gx, gy = lax.axis_index("gx"), lax.axis_index("gy")
    height, width = b_hbm.shape
    groups = width // L
    sketch_dim = rows_hbm.shape[0]
    last = groups
    block = 128
    blocks = height // block

    loads = []
    for a, src in enumerate((b_hbm, dx_hbm, dy_hbm)):
        for p in range(groups):
            copy = pltpu.make_async_copy(
                src.at[:, pl.ds(p * L, L)], ext.at[a, p, pl.ds(PAD, height), :], in_sem.at[a * groups + p])
            copy.start()
            loads.append(copy)
    for s, (src, dst) in enumerate(((cols_hbm, cols_v), (rows_hbm, rows_v))):
        copy = pltpu.make_async_copy(src, dst, in_sem.at[3 * groups + s])
        copy.start()
        loads.append(copy)

    def device(ox, oy):
        return {"gx": lax.rem(gx + (ox + nx), nx), "gy": lax.rem(gy + (oy + ny), ny)}

    peers = {(sx % nx, sy % ny) for sx, sy in SIDES}
    peers |= {(o, 0) for o in range(1, nx)} | {(0, o) for o in range(1, ny)}
    barrier = pltpu.get_barrier_semaphore()
    for ox, oy in sorted(peers):
        pl.semaphore_signal(barrier, inc=1, device_id=device(ox, oy), device_id_type=MESH)

    lane = lax.broadcasted_iota(jnp.int32, (EDGE, L), 1)
    tall_lane = lax.broadcasted_iota(jnp.int32, (height, L), 1)
    one, zero = jnp.float32(1.0), jnp.float32(0.0)
    has_up = jnp.where(gx > 0, one, zero)
    has_down = jnp.where(gx < nx - 1, one, zero)
    has_left = jnp.where(gy > 0, one, zero)
    has_right = jnp.where(gy < ny - 1, one, zero)
    col_mask = jnp.where(lane < L // 2, has_right, has_left)
    empty = jnp.zeros((EDGE, L), jnp.float32)
    bottom = PAD + height
    for p in range(groups + 1):
        for at in (0, bottom + EDGE):
            ext[0, p, pl.ds(at, EDGE), :] = empty
            for k in range(ITERS - 1):
                basis[k, p, pl.ds(at, EDGE), :] = empty
    part[...] = jnp.zeros_like(part)

    for copy in loads[: 3 * groups]:
        copy.wait()
    for a in range(3):
        packed = jnp.where(
            tall_lane < L // 2, ext[a, 0, pl.ds(PAD, height), :], ext[a, groups - 1, pl.ds(PAD, height), :])
        diag_out[0, a] = packed[:EDGE]
        diag_out[1, a] = packed[height - EDGE:]
        turned = jnp.transpose(packed)
        col_out[0, a] = turned[:EDGE]
        col_out[1, a] = turned[L - EDGE:]
    pl.semaphore_wait(barrier, len(peers))

    sends = []
    for d, (sx, sy) in enumerate(SIDES):
        if sy == 0:
            src_at, dst_at = (PAD, bottom) if sx < 0 else (bottom - EDGE, PAD - EDGE)
            src = ext.at[:, pl.ds(0, groups), pl.ds(src_at, EDGE), :]
            dst = ext.at[:, pl.ds(0, groups), pl.ds(dst_at, EDGE), :]
        elif sx == 0:
            src, dst = col_out.at[int(sy > 0)], col_in.at[int(sy > 0)]
        else:
            src, dst = diag_out.at[int(sx > 0)], diag_in.at[d - 4]
        copy = pltpu.make_async_remote_copy(
            src_ref=src, dst_ref=dst, send_sem=hs_sem.at[d], recv_sem=hr_sem.at[d],
            device_id=device(sx, sy), device_id_type=MESH)
        copy.start()
        sends.append(copy)

    for copy in loads[3 * groups:]:
        copy.wait()
    turned_cols = jnp.transpose(cols_v[...])
    high = turned_cols.astype(jnp.bfloat16)
    ct_hi[...] = high
    ct_lo[...] = (turned_cols - high.astype(jnp.float32)).astype(jnp.bfloat16)
    rows_t[...] = jnp.transpose(rows_v[...])

    def sketch_block(view, i):
        field = jnp.concatenate(
            [view[p, pl.ds(PAD + i * block, block), :] for p in range(groups)], axis=1)
        hi = field.astype(jnp.bfloat16)
        lo = (field - hi.astype(jnp.float32)).astype(jnp.bfloat16)
        dot = lambda u, v: jnp.dot(u, v, preferred_element_type=jnp.float32)
        product = dot(hi, ct_hi[...]) + dot(hi, ct_lo[...]) + dot(lo, ct_hi[...])
        product = product * rows_t[pl.ds(i * block, block), :]
        return jnp.sum(product.reshape(block // 8, 8, sketch_dim), axis=0)

    def view_of(k):
        return ext.at[0] if k == 0 else basis.at[k - 1]

    def stencil(k, at, row_mask=None):
        src, out = view_of(k - 1), view_of(k)
        mid = [src[p, pl.ds(at, EDGE), :] for p in range(groups + 1)]
        from_left = [pltpu.roll(v, 1, 1) for v in mid]
        from_right = [pltpu.roll(v, L - 1, 1) for v in mid]
        for p in range(groups + 1 if k < ITERS else groups):
            left = jnp.where(lane == 0, from_left[p - 1], from_left[p])
            right = jnp.where(lane == L - 1, from_right[(p + 1) % (groups + 1)], from_right[p])
            up = src[p, pl.ds(at - 1, EDGE), :]
            down = src[p, pl.ds(at + 1, EDGE), :]
            total = (up + down) + ext[1, p, pl.ds(at, EDGE), :] * (up - down)
            total = total + ((left + right) + ext[2, p, pl.ds(at, EDGE), :] * (left - right))
            value = -0.5 * total
            if k >= 2:
                value = value - view_of(k - 2)[p, pl.ds(at, EDGE), :]
            if p == last:
                value = value * col_mask
            if row_mask is not None:
                value = value * row_mask
            out[p, pl.ds(at, EDGE), :] = value

    def close(k, total):
        part[pl.ds(k, 1), :] = jnp.sum(total, axis=0, keepdims=True)

    nothing = jnp.zeros((8, sketch_dim), jnp.float32)
    close(0, lax.fori_loop(0, blocks, lambda i, t: t + sketch_block(view_of(0), i), nothing))

    for copy in sends:
        copy.wait()
    gap = jnp.zeros((L - 2 * EDGE, height), jnp.float32)
    for a in range(3):
        beside = jnp.transpose(jnp.concatenate([col_in[0, a], gap, col_in[1, a]], axis=0))
        if a == 0:
            beside = beside * jnp.where(tall_lane < L // 2, has_right, has_left)
        ext[a, last, pl.ds(PAD, height), :] = beside
        above = jnp.where(lane < L // 2, diag_in[2, a], diag_in[3, a])
        below = jnp.where(lane < L // 2, diag_in[0, a], diag_in[1, a])
        if a == 0:
            above, below = above * col_mask, below * col_mask
        ext[a, last, pl.ds(PAD - EDGE, EDGE), :] = above
        ext[a, last, pl.ds(bottom, EDGE), :] = below
    for p in range(groups + 1):
        ext[0, p, pl.ds(PAD - EDGE, EDGE), :] = ext[0, p, pl.ds(PAD - EDGE, EDGE), :] * has_up
        ext[0, p, pl.ds(bottom, EDGE), :] = ext[0, p, pl.ds(bottom, EDGE), :] * has_down

    for k in range(1, ITERS + 1):
        if k < ITERS:
            stencil(k, PAD - EDGE, has_up)
            stencil(k, bottom, has_down)

        def step(i, total, k=k):
            for s in range(block // EDGE):
                stencil(k, PAD + i * block + s * EDGE)
            return total + sketch_block(view_of(k - 1), i) if k >= 2 else total

        total = lax.fori_loop(0, blocks, step, nothing)
        if k >= 2:
            close(k - 1, total)
    close(ITERS, lax.fori_loop(0, blocks, lambda i, t: t + sketch_block(view_of(ITERS), i), nothing))

    def exchange(src, got, send, recv, count, along):
        copies = []
        for o in range(1, count):
            copy = pltpu.make_async_remote_copy(
                src_ref=src, dst_ref=got.at[o - 1], send_sem=send.at[o - 1], recv_sem=recv.at[o - 1],
                device_id=device(*((o, 0) if along == 0 else (0, o))), device_id_type=MESH)
            copy.start()
            copies.append(copy)
        for copy in copies:
            copy.wait()
        total = src[...]
        for o in range(1, count):
            total = total + got[o - 1]
        return total

    sum_x[...] = exchange(part, got_x, xs_sem, xr_sem, nx, 0)
    whole = exchange(sum_x, got_y, ys_sem, yr_sem, ny, 1)

    gram = {}
    for a in range(ITERS + 1):
        for c in range(a, ITERS + 1):
            entry = jnp.sum(whole[a:a + 1] * whole[c:c + 1], axis=1, keepdims=True)
            gram[a, c] = jnp.broadcast_to(entry, (EDGE, L))
    y, res = solve_small(gram)

    def combine(i, _):
        for p in range(groups):
            for s in range(4):
                at = i * 32 + s * EDGE
                v = [view_of(k)[p, pl.ds(PAD + at, EDGE), :] for k in range(ITERS + 1)]
                x, r = y[0] * v[0], res[0] * v[0]
                for k in range(1, ITERS + 1):
                    if k < ITERS:
                        x = x + y[k] * v[k]
                    r = r + res[k] * v[k]
                x_v[p, pl.ds(at, EDGE), :] = x
                r_v[p, pl.ds(at, EDGE), :] = r
        return 0

    stores = []
    for q in range(blocks):
        lax.fori_loop(q * (block // 32), (q + 1) * (block // 32), combine, 0)
        for o, (src, dst) in enumerate(((x_v, x_hbm), (r_v, r_hbm))):
            for p in range(groups):
                copy = pltpu.make_async_copy(
                    src.at[p, pl.ds(q * block, block), :],
                    dst.at[pl.ds(q * block, block), pl.ds(p * L, L)],
                    out_sem.at[(q * 2 + o) * groups + p])
                copy.start()
                stores.append(copy)
    for copy in stores:
        copy.wait()


def solution(mesh):
    nx, ny = mesh.shape["gx"], mesh.shape["gy"]

    def body(right_side, drift_x, drift_y, sketch_rows, sketch_cols):
        height, width = right_side.shape
        groups = width // L
        dim = sketch_rows.shape[0]
        tall = height + 2 * PAD
        f32, bf16 = jnp.float32, jnp.bfloat16
        dma = pltpu.SemaphoreType.DMA
        out = jax.ShapeDtypeStruct((height, width), f32)
        return pl.pallas_call(
            lambda *refs: kernel(nx, ny, *refs),
            out_shape=(out, out),
            in_specs=[pl.BlockSpec(memory_space=pl.ANY)] * 5,
            out_specs=[pl.BlockSpec(memory_space=pl.ANY)] * 2,
            scratch_shapes=[
                pltpu.VMEM((3, groups + 1, tall, L), f32),
                pltpu.VMEM((ITERS, groups + 1, tall, L), f32),
                pltpu.VMEM((dim, height), f32),
                pltpu.VMEM((dim, width), f32),
                pltpu.VMEM((height, dim), f32),
                pltpu.VMEM((width, dim), bf16),
                pltpu.VMEM((width, dim), bf16),
                pltpu.VMEM((2, 3, EDGE, height), f32),
                pltpu.VMEM((2, 3, EDGE, height), f32),
                pltpu.VMEM((2, 3, EDGE, L), f32),
                pltpu.VMEM((4, 3, EDGE, L), f32),
                pltpu.VMEM((8, dim), f32),
                pltpu.VMEM((nx - 1, 8, dim), f32),
                pltpu.VMEM((8, dim), f32),
                pltpu.VMEM((ny - 1, 8, dim), f32),
                pltpu.VMEM((groups, height, L), f32),
                pltpu.VMEM((groups, height, L), f32),
                dma((3 * groups + 2,)),
                dma((2 * groups * (height // 128),)),
                dma((8,)), dma((8,)),
                dma((nx - 1,)), dma((nx - 1,)),
                dma((ny - 1,)), dma((ny - 1,)),
            ],
            compiler_params=pltpu.CompilerParams(
                collective_id=0, has_side_effects=True, vmem_limit_bytes=48 * 1024 * 1024),
        )(right_side, drift_x, drift_y, sketch_rows, sketch_cols)

    in_specs = (P("gx", "gy"), P("gx", "gy"), P("gx", "gy"), P(None, "gx"), P(None, "gy"))
    out_specs = (P("gx", "gy"), P("gx", "gy"))
    return jax.shard_map(body, mesh=mesh, in_specs=in_specs, out_specs=out_specs, check_vma=False)
```

```python
import jax
import jax.numpy as jnp
from jax import lax
from jax.experimental import pallas as pl
from jax.experimental.pallas import tpu as pltpu
from jax.sharding import PartitionSpec as P

ITERS = 4
CENTER = 4.0 + 0.05
L = 128
PAD = 16
EDGE = 8
MESH = pl.DeviceIdType.MESH
SIDES = [(-1, 0), (1, 0), (0, -1), (0, 1), (-1, -1), (-1, 1), (1, -1), (1, 1)]


def solve_small(gram):
    n = ITERS

    def g(a, b):
        return gram[(min(a, b), max(a, b))]

    f = {}
    for a in range(n + 1):
        for j in range(n):
            value = CENTER * g(a, j) + 2.0 * g(a, j + 1)
            f[a, j] = value + 2.0 * g(a, j - 1) if j else value
    m = {}
    for i in range(n):
        for j in range(i + 1):
            value = CENTER * f[i, j] + 2.0 * f[i + 1, j]
            m[i, j] = value + 2.0 * f[i - 1, j] if i else value
    inv, low, scaled = [], {}, {}
    for j in range(n):
        for i in range(j, n):
            acc = m[i, j]
            for k in range(j):
                acc = acc - scaled[i, k] * low[j, k]
            scaled[i, j] = acc
        inv.append(1.0 / scaled[j, j])
        for i in range(j + 1, n):
            low[i, j] = scaled[i, j] * inv[j]
    forward = []
    for i in range(n):
        acc = f[0, i]
        for k in range(i):
            acc = acc - low[i, k] * forward[k]
        forward.append(acc)
    y = [None] * n
    for i in reversed(range(n)):
        acc = forward[i] * inv[i]
        for k in range(i + 1, n):
            acc = acc - low[k, i] * y[k]
        y[i] = acc
    res = []
    for k in range(n + 1):
        z = 0.0
        if k < n:
            z = z + CENTER * y[k]
        if k >= 1:
            z = z + 2.0 * y[k - 1]
        if k + 1 < n:
            z = z + 2.0 * y[k + 1]
        res.append(1.0 - z if k == 0 else -z)
    return y, res


def kernel(nx, ny, b_hbm, dx_hbm, dy_hbm, rows_hbm, cols_hbm, basis_all, coefs,
           ext, rows_v, cols_v, rows_t, ct_hi, ct_lo, col_out, col_in, diag_out, diag_in,
           part, got_x, sum_x, got_y, in_sem, hs_sem, hr_sem, xs_sem, xr_sem, ys_sem, yr_sem):
    gx, gy = lax.axis_index("gx"), lax.axis_index("gy")
    height, width = b_hbm.shape
    groups = width // L
    sketch_dim = rows_hbm.shape[0]
    last = groups
    block = 128
    blocks = height // block
    basis = basis_all.at[pl.ds(1, ITERS)]

    loads = []
    for a, src in enumerate((b_hbm, dx_hbm, dy_hbm)):
        for p in range(groups):
            copy = pltpu.make_async_copy(
                src.at[:, pl.ds(p * L, L)], ext.at[a, p, pl.ds(PAD, height), :], in_sem.at[a * groups + p])
            copy.start()
            loads.append(copy)
    for s, (src, dst) in enumerate(((cols_hbm, cols_v), (rows_hbm, rows_v))):
        copy = pltpu.make_async_copy(src, dst, in_sem.at[3 * groups + s])
        copy.start()
        loads.append(copy)

    def device(ox, oy):
        return {"gx": lax.rem(gx + (ox + nx), nx), "gy": lax.rem(gy + (oy + ny), ny)}

    peers = {(sx % nx, sy % ny) for sx, sy in SIDES}
    peers |= {(o, 0) for o in range(1, nx)} | {(0, o) for o in range(1, ny)}
    barrier = pltpu.get_barrier_semaphore()
    for ox, oy in sorted(peers):
        pl.semaphore_signal(barrier, inc=1, device_id=device(ox, oy), device_id_type=MESH)

    lane = lax.broadcasted_iota(jnp.int32, (EDGE, L), 1)
    tall_lane = lax.broadcasted_iota(jnp.int32, (height, L), 1)
    one, zero = jnp.float32(1.0), jnp.float32(0.0)
    has_up = jnp.where(gx > 0, one, zero)
    has_down = jnp.where(gx < nx - 1, one, zero)
    has_left = jnp.where(gy > 0, one, zero)
    has_right = jnp.where(gy < ny - 1, one, zero)
    col_mask = jnp.where(lane < L // 2, has_right, has_left)
    empty = jnp.zeros((EDGE, L), jnp.float32)
    bottom = PAD + height
    for p in range(groups + 1):
        for at in (0, bottom + EDGE):
            ext[0, p, pl.ds(at, EDGE), :] = empty
            for k in range(ITERS - 1):
                basis[k, p, pl.ds(at, EDGE), :] = empty
    part[...] = jnp.zeros_like(part)

    for copy in loads[: 3 * groups]:
        copy.wait()
    keep = pltpu.make_async_copy(
        ext.at[0, pl.ds(0, groups), pl.ds(PAD, height), :],
        basis_all.at[0, pl.ds(0, groups), pl.ds(PAD, height), :], in_sem.at[3 * groups + 2])
    keep.start()
    for a in range(3):
        packed = jnp.where(
            tall_lane < L // 2, ext[a, 0, pl.ds(PAD, height), :], ext[a, groups - 1, pl.ds(PAD, height), :])
        diag_out[0, a] = packed[:EDGE]
        diag_out[1, a] = packed[height - EDGE:]
        turned = jnp.transpose(packed)
        col_out[0, a] = turned[:EDGE]
        col_out[1, a] = turned[L - EDGE:]
    pl.semaphore_wait(barrier, len(peers))

    sends = []
    for d, (sx, sy) in enumerate(SIDES):
        if sy == 0:
            src_at, dst_at = (PAD, bottom) if sx < 0 else (bottom - EDGE, PAD - EDGE)
            src = ext.at[:, pl.ds(0, groups), pl.ds(src_at, EDGE), :]
            dst = ext.at[:, pl.ds(0, groups), pl.ds(dst_at, EDGE), :]
        elif sx == 0:
            src, dst = col_out.at[int(sy > 0)], col_in.at[int(sy > 0)]
        else:
            src, dst = diag_out.at[int(sx > 0)], diag_in.at[d - 4]
        copy = pltpu.make_async_remote_copy(
            src_ref=src, dst_ref=dst, send_sem=hs_sem.at[d], recv_sem=hr_sem.at[d],
            device_id=device(sx, sy), device_id_type=MESH)
        copy.start()
        sends.append(copy)

    for copy in loads[3 * groups:]:
        copy.wait()
    turned_cols = jnp.transpose(cols_v[...])
    high = turned_cols.astype(jnp.bfloat16)
    ct_hi[...] = high
    ct_lo[...] = (turned_cols - high.astype(jnp.float32)).astype(jnp.bfloat16)
    rows_t[...] = jnp.transpose(rows_v[...])

    def sketch_block(view, i):
        field = jnp.concatenate(
            [view[p, pl.ds(PAD + i * block, block), :] for p in range(groups)], axis=1)
        hi = field.astype(jnp.bfloat16)
        lo = (field - hi.astype(jnp.float32)).astype(jnp.bfloat16)
        dot = lambda u, v: jnp.dot(u, v, preferred_element_type=jnp.float32)
        product = dot(hi, ct_hi[...]) + dot(hi, ct_lo[...]) + dot(lo, ct_hi[...])
        product = product * rows_t[pl.ds(i * block, block), :]
        return jnp.sum(product.reshape(block // 8, 8, sketch_dim), axis=0)

    def view_of(k):
        return ext.at[0] if k == 0 else basis.at[k - 1]

    def stencil(k, at, row_mask=None):
        src, out = view_of(k - 1), view_of(k)
        mid = [src[p, pl.ds(at, EDGE), :] for p in range(groups + 1)]
        from_left = [pltpu.roll(v, 1, 1) for v in mid]
        from_right = [pltpu.roll(v, L - 1, 1) for v in mid]
        for p in range(groups + 1 if k < ITERS else groups):
            left = jnp.where(lane == 0, from_left[p - 1], from_left[p])
            right = jnp.where(lane == L - 1, from_right[(p + 1) % (groups + 1)], from_right[p])
            up = src[p, pl.ds(at - 1, EDGE), :]
            down = src[p, pl.ds(at + 1, EDGE), :]
            total = (up + down) + ext[1, p, pl.ds(at, EDGE), :] * (up - down)
            total = total + ((left + right) + ext[2, p, pl.ds(at, EDGE), :] * (left - right))
            value = -0.5 * total
            if k >= 2:
                value = value - view_of(k - 2)[p, pl.ds(at, EDGE), :]
            if p == last:
                value = value * col_mask
            if row_mask is not None:
                value = value * row_mask
            out[p, pl.ds(at, EDGE), :] = value

    def close(k, total):
        part[pl.ds(k, 1), :] = jnp.sum(total, axis=0, keepdims=True)

    nothing = jnp.zeros((8, sketch_dim), jnp.float32)
    close(0, lax.fori_loop(0, blocks, lambda i, t: t + sketch_block(view_of(0), i), nothing))

    for copy in sends:
        copy.wait()
    gap = jnp.zeros((L - 2 * EDGE, height), jnp.float32)
    for a in range(3):
        beside = jnp.transpose(jnp.concatenate([col_in[0, a], gap, col_in[1, a]], axis=0))
        if a == 0:
            beside = beside * jnp.where(tall_lane < L // 2, has_right, has_left)
        ext[a, last, pl.ds(PAD, height), :] = beside
        above = jnp.where(lane < L // 2, diag_in[2, a], diag_in[3, a])
        below = jnp.where(lane < L // 2, diag_in[0, a], diag_in[1, a])
        if a == 0:
            above, below = above * col_mask, below * col_mask
        ext[a, last, pl.ds(PAD - EDGE, EDGE), :] = above
        ext[a, last, pl.ds(bottom, EDGE), :] = below
    for p in range(groups + 1):
        ext[0, p, pl.ds(PAD - EDGE, EDGE), :] = ext[0, p, pl.ds(PAD - EDGE, EDGE), :] * has_up
        ext[0, p, pl.ds(bottom, EDGE), :] = ext[0, p, pl.ds(bottom, EDGE), :] * has_down

    for k in range(1, ITERS + 1):
        if k < ITERS:
            stencil(k, PAD - EDGE, has_up)
            stencil(k, bottom, has_down)

        def step(i, total, k=k):
            for s in range(block // EDGE):
                stencil(k, PAD + i * block + s * EDGE)
            return total + sketch_block(view_of(k - 1), i) if k >= 2 else total

        total = lax.fori_loop(0, blocks, step, nothing)
        if k >= 2:
            close(k - 1, total)
    close(ITERS, lax.fori_loop(0, blocks, lambda i, t: t + sketch_block(view_of(ITERS), i), nothing))

    def exchange(src, got, send, recv, count, along):
        copies = []
        for o in range(1, count):
            copy = pltpu.make_async_remote_copy(
                src_ref=src, dst_ref=got.at[o - 1], send_sem=send.at[o - 1], recv_sem=recv.at[o - 1],
                device_id=device(*((o, 0) if along == 0 else (0, o))), device_id_type=MESH)
            copy.start()
            copies.append(copy)
        for copy in copies:
            copy.wait()
        total = src[...]
        for o in range(1, count):
            total = total + got[o - 1]
        return total

    sum_x[...] = exchange(part, got_x, xs_sem, xr_sem, nx, 0)
    whole = exchange(sum_x, got_y, ys_sem, yr_sem, ny, 1)

    gram = {}
    for a in range(ITERS + 1):
        for c in range(a, ITERS + 1):
            entry = jnp.sum(whole[a:a + 1] * whole[c:c + 1], axis=1, keepdims=True)
            gram[a, c] = jnp.broadcast_to(entry, (EDGE, L))
    y, res = solve_small(gram)
    for k, value in enumerate(y + res):
        coefs[k] = value
    keep.wait()


def combine(basis, coefs, x_hbm, r_hbm, x_v, r_v, sem):
    groups, height = x_v.shape[0], x_v.shape[1]
    block = 128

    def rows(i, _):
        y = [coefs[k] for k in range(ITERS)]
        res = [coefs[ITERS + k] for k in range(ITERS + 1)]
        for p in range(groups):
            for s in range(4):
                at = i * 32 + s * EDGE
                v = [basis[k, p, pl.ds(PAD + at, EDGE), :] for k in range(ITERS + 1)]
                x, r = y[0] * v[0], res[0] * v[0]
                for k in range(1, ITERS + 1):
                    if k < ITERS:
                        x = x + y[k] * v[k]
                    r = r + res[k] * v[k]
                x_v[p, pl.ds(at, EDGE), :] = x
                r_v[p, pl.ds(at, EDGE), :] = r
        return 0

    stores = []
    for q in range(height // block):
        lax.fori_loop(q * (block // 32), (q + 1) * (block // 32), rows, 0)
        for o, (src, dst) in enumerate(((x_v, x_hbm), (r_v, r_hbm))):
            for p in range(groups):
                copy = pltpu.make_async_copy(
                    src.at[p, pl.ds(q * block, block), :],
                    dst.at[pl.ds(q * block, block), pl.ds(p * L, L)],
                    sem.at[(q * 2 + o) * groups + p])
                copy.start()
                stores.append(copy)
    for copy in stores:
        copy.wait()


def solution(mesh):
    nx, ny = mesh.shape["gx"], mesh.shape["gy"]

    def body(right_side, drift_x, drift_y, sketch_rows, sketch_cols):
        height, width = right_side.shape
        groups = width // L
        dim = sketch_rows.shape[0]
        tall = height + 2 * PAD
        f32, bf16 = jnp.float32, jnp.bfloat16
        dma = pltpu.SemaphoreType.DMA
        pieces = height // 128
        hbm = pltpu.HBM((height, width), f32)
        args = [pltpu.with_memory_space_constraint(v, pltpu.HBM)
                for v in (right_side, drift_x, drift_y, sketch_rows, sketch_cols)]
        basis, coefs = pl.pallas_call(
            lambda *refs: kernel(nx, ny, *refs),
            out_shape=(
                pltpu.VMEM((ITERS + 1, groups + 1, tall, L), f32), pltpu.VMEM((2 * ITERS + 1, EDGE, L), f32)),
            in_specs=[pl.BlockSpec(memory_space=pltpu.HBM)] * 5,
            out_specs=[pl.BlockSpec(memory_space=pltpu.VMEM)] * 2,
            scratch_shapes=[
                pltpu.VMEM((3, groups + 1, tall, L), f32),
                pltpu.VMEM((dim, height), f32),
                pltpu.VMEM((dim, width), f32),
                pltpu.VMEM((height, dim), f32),
                pltpu.VMEM((width, dim), bf16),
                pltpu.VMEM((width, dim), bf16),
                pltpu.VMEM((2, 3, EDGE, height), f32),
                pltpu.VMEM((2, 3, EDGE, height), f32),
                pltpu.VMEM((2, 3, EDGE, L), f32),
                pltpu.VMEM((4, 3, EDGE, L), f32),
                pltpu.VMEM((8, dim), f32),
                pltpu.VMEM((nx - 1, 8, dim), f32),
                pltpu.VMEM((8, dim), f32),
                pltpu.VMEM((ny - 1, 8, dim), f32),
                dma((3 * groups + 3,)),
                dma((8,)), dma((8,)),
                dma((nx - 1,)), dma((nx - 1,)),
                dma((ny - 1,)), dma((ny - 1,)),
            ],
            compiler_params=pltpu.CompilerParams(
                collective_id=0, has_side_effects=True, vmem_limit_bytes=40 * 1024 * 1024),
        )(*args)
        return pl.pallas_call(
            combine,
            out_shape=(hbm, hbm),
            in_specs=[pl.BlockSpec(memory_space=pltpu.VMEM)] * 2,
            out_specs=[pl.BlockSpec(memory_space=pltpu.HBM)] * 2,
            scratch_shapes=[
                pltpu.VMEM((groups, height, L), f32), pltpu.VMEM((groups, height, L), f32),
                dma((2 * groups * pieces,))],
            compiler_params=pltpu.CompilerParams(vmem_limit_bytes=8 * 1024 * 1024),
        )(basis, coefs)

    in_specs = (P("gx", "gy"), P("gx", "gy"), P("gx", "gy"), P(None, "gx"), P(None, "gy"))
    out_specs = (P("gx", "gy"), P("gx", "gy"))
    return jax.shard_map(body, mesh=mesh, in_specs=in_specs, out_specs=out_specs, check_vma=False)
```

```python
import jax
import jax.numpy as jnp
from jax import lax
from jax.experimental import pallas as pl
from jax.experimental.pallas import tpu as pltpu
from jax.sharding import PartitionSpec as P

ITERS = 4
CENTER = 4.0 + 0.05
L = 128
PAD = 16
EDGE = 8
MESH = pl.DeviceIdType.MESH
PIECES = [pl.ds(0, ITERS - 1), pl.ds(8, 2)]
SIDES = [(-1, 0), (1, 0), (0, -1), (0, 1), (-1, -1), (-1, 1), (1, -1), (1, 1)]


def solve_small(gram):
    n = ITERS

    def g(a, b):
        return gram[(min(a, b), max(a, b))]

    f = {}
    for a in range(n + 1):
        for j in range(n):
            value = CENTER * g(a, j) + 2.0 * g(a, j + 1)
            f[a, j] = value + 2.0 * g(a, j - 1) if j else value
    m = {}
    for i in range(n):
        for j in range(i + 1):
            value = CENTER * f[i, j] + 2.0 * f[i + 1, j]
            m[i, j] = value + 2.0 * f[i - 1, j] if i else value
    inv, low, scaled = [], {}, {}
    for j in range(n):
        for i in range(j, n):
            acc = m[i, j]
            for k in range(j):
                acc = acc - scaled[i, k] * low[j, k]
            scaled[i, j] = acc
        inv.append(1.0 / scaled[j, j])
        for i in range(j + 1, n):
            low[i, j] = scaled[i, j] * inv[j]
    forward = []
    for i in range(n):
        acc = f[0, i]
        for k in range(i):
            acc = acc - low[i, k] * forward[k]
        forward.append(acc)
    y = [None] * n
    for i in reversed(range(n)):
        acc = forward[i] * inv[i]
        for k in range(i + 1, n):
            acc = acc - low[k, i] * y[k]
        y[i] = acc
    res = []
    for k in range(n + 1):
        z = 0.0
        if k < n:
            z = z + CENTER * y[k]
        if k >= 1:
            z = z + 2.0 * y[k - 1]
        if k + 1 < n:
            z = z + 2.0 * y[k + 1]
        res.append(1.0 - z if k == 0 else -z)
    return y, res


def kernel(nx, ny, b_hbm, dx_hbm, dy_hbm, rows_hbm, cols_hbm, basis_all, coefs,
           ext, rows_v, cols_v, rows_t, ct_hi, ct_lo, col_out, col_in, diag_out, diag_in,
           part, got_x, sum_x, got_y, in_sem, hs_sem, hr_sem, xs_sem, xr_sem, ys_sem, yr_sem):
    gx, gy = lax.axis_index("gx"), lax.axis_index("gy")
    height, width = b_hbm.shape
    groups = width // L
    sketch_dim = rows_hbm.shape[0]
    last = groups
    block = 128
    blocks = height // block
    basis = basis_all.at[pl.ds(1, ITERS)]

    loads = []
    order = [0, groups - 1] + list(range(1, groups - 1))
    for p in order:
        for a, src in enumerate((b_hbm, dx_hbm, dy_hbm)):
            copy = pltpu.make_async_copy(
                src.at[:, pl.ds(p * L, L)], ext.at[a, p, pl.ds(PAD, height), :], in_sem.at[a * groups + p])
            copy.start()
            loads.append(copy)
    for s, (src, dst) in enumerate(((cols_hbm, cols_v), (rows_hbm, rows_v))):
        copy = pltpu.make_async_copy(src, dst, in_sem.at[3 * groups + s])
        copy.start()
        loads.append(copy)

    def device(ox, oy):
        return {"gx": lax.rem(gx + (ox + nx), nx), "gy": lax.rem(gy + (oy + ny), ny)}

    peers = {(sx % nx, sy % ny) for sx, sy in SIDES}
    peers |= {(o, 0) for o in range(1, nx)} | {(0, o) for o in range(1, ny)}
    barrier = pltpu.get_barrier_semaphore()
    lane = lax.broadcasted_iota(jnp.int32, (EDGE, L), 1)
    tall_lane = lax.broadcasted_iota(jnp.int32, (height, L), 1)
    one, zero = jnp.float32(1.0), jnp.float32(0.0)
    has_up = jnp.where(gx > 0, one, zero)
    has_down = jnp.where(gx < nx - 1, one, zero)
    has_left = jnp.where(gy > 0, one, zero)
    has_right = jnp.where(gy < ny - 1, one, zero)
    col_mask = jnp.where(lane < L // 2, has_right, has_left)
    empty = jnp.zeros((EDGE, L), jnp.float32)
    bottom = PAD + height
    diag_in[...] = jnp.zeros_like(diag_in)
    col_in[...] = jnp.zeros_like(col_in)
    for p in range(groups):
        for a in range(3):
            ext[a, p, pl.ds(PAD - EDGE, EDGE), :] = empty
            ext[a, p, pl.ds(bottom, EDGE), :] = empty
    for ox, oy in sorted(peers):
        pl.semaphore_signal(barrier, inc=1, device_id=device(ox, oy), device_id_type=MESH)

    for p in range(groups + 1):
        for at in (0, bottom + EDGE):
            ext[0, p, pl.ds(at, EDGE), :] = empty
            for k in range(ITERS - 1):
                basis[k, p, pl.ds(at, EDGE), :] = empty
    part[...] = jnp.zeros_like(part)

    for copy in loads[:6]:
        copy.wait()
    for a in range(3):
        packed = jnp.where(
            tall_lane < L // 2, ext[a, 0, pl.ds(PAD, height), :], ext[a, groups - 1, pl.ds(PAD, height), :])
        diag_out[0, a] = packed[:EDGE]
        diag_out[1, a] = packed[height - EDGE:]
        turned = jnp.transpose(packed)
        col_out[0, a] = turned[:EDGE]
        col_out[1, a] = turned[L - EDGE:]
    pl.semaphore_wait(barrier, len(peers))

    def inside(sx, sy):
        return (gx + sx >= 0) & (gx + sx < nx) & (gy + sy >= 0) & (gy + sy < ny)

    sends = []
    for d, (sx, sy) in reversed(list(enumerate(SIDES))):
        if sy == 0:
            src_at, dst_at = (PAD, bottom) if sx < 0 else (bottom - EDGE, PAD - EDGE)
            src = ext.at[:, pl.ds(0, groups), pl.ds(src_at, EDGE), :]
            dst = ext.at[:, pl.ds(0, groups), pl.ds(dst_at, EDGE), :]
        elif sx == 0:
            src, dst = col_out.at[int(sy > 0)], col_in.at[int(sy > 0)]
        else:
            src, dst = diag_out.at[int(sx > 0)], diag_in.at[d - 4]
        copy = pltpu.make_async_remote_copy(
            src_ref=src, dst_ref=dst, send_sem=hs_sem.at[d], recv_sem=hr_sem.at[d],
            device_id=device(sx, sy), device_id_type=MESH)
        if d == 1:
            for load in loads[6:3 * groups]:
                load.wait()
        pl.when(inside(sx, sy))(copy.start)
        sends.append((copy, sx, sy))
    keep = pltpu.make_async_copy(
        ext.at[0, pl.ds(0, groups), pl.ds(PAD, height), :],
        basis_all.at[0, pl.ds(0, groups), pl.ds(PAD, height), :], in_sem.at[3 * groups + 2])
    keep.start()

    for copy in loads[3 * groups:]:
        copy.wait()
    turned_cols = jnp.transpose(cols_v[...])
    high = turned_cols.astype(jnp.bfloat16)
    ct_hi[...] = high
    ct_lo[...] = (turned_cols - high.astype(jnp.float32)).astype(jnp.bfloat16)
    rows_t[...] = jnp.transpose(rows_v[...])

    def sketch_block(view, i):
        field = jnp.concatenate(
            [view[p, pl.ds(PAD + i * block, block), :] for p in range(groups)], axis=1)
        hi = field.astype(jnp.bfloat16)
        lo = (field - hi.astype(jnp.float32)).astype(jnp.bfloat16)
        dot = lambda u, v: jnp.dot(u, v, preferred_element_type=jnp.float32)
        product = dot(hi, ct_hi[...]) + dot(hi, ct_lo[...]) + dot(lo, ct_hi[...])
        product = product * rows_t[pl.ds(i * block, block), :]
        return jnp.sum(product.reshape(block // 8, 8, sketch_dim), axis=0)

    def view_of(k):
        return ext.at[0] if k == 0 else basis.at[k - 1]

    def stencil(k, at, row_mask=None):
        src, out = view_of(k - 1), view_of(k)
        mid = [src[p, pl.ds(at, EDGE), :] for p in range(groups + 1)]
        from_left = [pltpu.roll(v, 1, 1) for v in mid]
        from_right = [pltpu.roll(v, L - 1, 1) for v in mid]
        for p in range(groups + 1 if k < ITERS else groups):
            left = jnp.where(lane == 0, from_left[p - 1], from_left[p])
            right = jnp.where(lane == L - 1, from_right[(p + 1) % (groups + 1)], from_right[p])
            up = src[p, pl.ds(at - 1, EDGE), :]
            down = src[p, pl.ds(at + 1, EDGE), :]
            total = (up + down) + ext[1, p, pl.ds(at, EDGE), :] * (up - down)
            total = total + ((left + right) + ext[2, p, pl.ds(at, EDGE), :] * (left - right))
            value = -0.5 * total
            if k >= 2:
                value = value - view_of(k - 2)[p, pl.ds(at, EDGE), :]
            if p == last:
                value = value * col_mask
            if row_mask is not None:
                value = value * row_mask
            out[p, pl.ds(at, EDGE), :] = value

    def close(k, total):
        part[pl.ds(k if k < ITERS - 1 else 8 + k - (ITERS - 1), 1), :] = jnp.sum(total, axis=0, keepdims=True)

    nothing = jnp.zeros((8, sketch_dim), jnp.float32)
    close(0, lax.fori_loop(0, blocks, lambda i, t: t + sketch_block(view_of(0), i), nothing))

    for copy, sx, sy in sends:
        pl.when(inside(-sx, -sy))(copy.wait_recv)
    for copy, sx, sy in sends:
        pl.when(inside(sx, sy))(copy.wait_send)
    gap = jnp.zeros((L - 2 * EDGE, height), jnp.float32)
    for a in range(3):
        beside = jnp.transpose(jnp.concatenate([col_in[0, a], gap, col_in[1, a]], axis=0))
        ext[a, last, pl.ds(PAD, height), :] = beside
        above = jnp.where(lane < L // 2, diag_in[2, a], diag_in[3, a])
        below = jnp.where(lane < L // 2, diag_in[0, a], diag_in[1, a])
        ext[a, last, pl.ds(PAD - EDGE, EDGE), :] = above
        ext[a, last, pl.ds(bottom, EDGE), :] = below
    def start(src, got, send, recv, count, along, piece):
        copies = []
        rows = PIECES[piece]
        for o in range(1, count):
            copy = pltpu.make_async_remote_copy(
                src_ref=src.at[rows], dst_ref=got.at[o - 1, rows],
                send_sem=send.at[piece, o - 1], recv_sem=recv.at[piece, o - 1],
                device_id=device(*((o, 0) if along == 0 else (0, o))), device_id_type=MESH)
            copy.start()
            copies.append(copy)
        return copies

    def finish(copies, src, got, piece):
        rows = PIECES[piece]
        for copy in copies:
            copy.wait()
        total = src[rows]
        for o in range(len(copies)):
            total = total + got[o, rows]
        return total

    def along_x(piece):
        return start(part, got_x, xs_sem, xr_sem, nx, 0, piece)

    def along_y(piece):
        return start(sum_x, got_y, ys_sem, yr_sem, ny, 1, piece)

    for k in range(1, ITERS + 1):
        if k < ITERS:
            stencil(k, PAD - EDGE, has_up)
            stencil(k, bottom, has_down)

        if k == ITERS:
            early = along_x(0)

        def step(i, total, k=k):
            for s in range(block // EDGE):
                stencil(k, PAD + i * block + s * EDGE)
            return total + sketch_block(view_of(k - 1), i) if k >= 2 else total

        total = lax.fori_loop(0, blocks, step, nothing)
        if k >= 2:
            close(k - 1, total)
    close(ITERS, lax.fori_loop(0, blocks, lambda i, t: t + sketch_block(view_of(ITERS), i), nothing))

    late = along_x(1)
    sum_x[PIECES[0]] = finish(early, part, got_x, 0)
    early = along_y(0)
    sum_x[PIECES[1]] = finish(late, part, got_x, 1)
    late = along_y(1)
    sums = finish(early, sum_x, got_y, 0), finish(late, sum_x, got_y, 1)
    whole = [piece[k:k + 1] for piece in sums for k in range(piece.shape[0])]

    gram = {}
    for a in range(ITERS + 1):
        for c in range(a, ITERS + 1):
            entry = jnp.sum(whole[a] * whole[c], axis=1, keepdims=True)
            gram[a, c] = jnp.broadcast_to(entry, (EDGE, L))
    y, res = solve_small(gram)
    for k, value in enumerate(y + res):
        coefs[k] = value
    keep.wait()


def combine(basis, coefs, x_hbm, r_hbm, x_v, r_v, sem):
    groups, height = x_v.shape[0], x_v.shape[1]
    block = 128

    def rows(i, _):
        y = [coefs[k] for k in range(ITERS)]
        res = [coefs[ITERS + k] for k in range(ITERS + 1)]
        for p in range(groups):
            for s in range(4):
                at = i * 32 + s * EDGE
                v = [basis[k, p, pl.ds(PAD + at, EDGE), :] for k in range(ITERS + 1)]
                x, r = y[0] * v[0], res[0] * v[0]
                for k in range(1, ITERS + 1):
                    if k < ITERS:
                        x = x + y[k] * v[k]
                    r = r + res[k] * v[k]
                x_v[p, pl.ds(at, EDGE), :] = x
                r_v[p, pl.ds(at, EDGE), :] = r
        return 0

    stores = []
    for q in range(height // block):
        lax.fori_loop(q * (block // 32), (q + 1) * (block // 32), rows, 0)
        for o, (src, dst) in enumerate(((x_v, x_hbm), (r_v, r_hbm))):
            for p in range(groups):
                copy = pltpu.make_async_copy(
                    src.at[p, pl.ds(q * block, block), :],
                    dst.at[pl.ds(q * block, block), pl.ds(p * L, L)],
                    sem.at[(q * 2 + o) * groups + p])
                copy.start()
                stores.append(copy)
    for copy in stores:
        copy.wait()


def solution(mesh):
    nx, ny = mesh.shape["gx"], mesh.shape["gy"]

    def body(right_side, drift_x, drift_y, sketch_rows, sketch_cols):
        height, width = right_side.shape
        groups = width // L
        dim = sketch_rows.shape[0]
        tall = height + 2 * PAD
        f32, bf16 = jnp.float32, jnp.bfloat16
        dma = pltpu.SemaphoreType.DMA
        pieces = height // 128
        hbm = pltpu.HBM((height, width), f32)
        args = [pltpu.with_memory_space_constraint(v, pltpu.HBM)
                for v in (right_side, drift_x, drift_y, sketch_rows, sketch_cols)]
        basis, coefs = pl.pallas_call(
            lambda *refs: kernel(nx, ny, *refs),
            out_shape=(
                pltpu.VMEM((ITERS + 1, groups + 1, tall, L), f32), pltpu.VMEM((2 * ITERS + 1, EDGE, L), f32)),
            in_specs=[pl.BlockSpec(memory_space=pltpu.HBM)] * 5,
            out_specs=[pl.BlockSpec(memory_space=pltpu.VMEM)] * 2,
            scratch_shapes=[
                pltpu.VMEM((3, groups + 1, tall, L), f32),
                pltpu.VMEM((dim, height), f32),
                pltpu.VMEM((dim, width), f32),
                pltpu.VMEM((height, dim), f32),
                pltpu.VMEM((width, dim), bf16),
                pltpu.VMEM((width, dim), bf16),
                pltpu.VMEM((2, 3, EDGE, height), f32),
                pltpu.VMEM((2, 3, EDGE, height), f32),
                pltpu.VMEM((2, 3, EDGE, L), f32),
                pltpu.VMEM((4, 3, EDGE, L), f32),
                pltpu.VMEM((16, dim), f32),
                pltpu.VMEM((nx - 1, 16, dim), f32),
                pltpu.VMEM((16, dim), f32),
                pltpu.VMEM((ny - 1, 16, dim), f32),
                dma((3 * groups + 3,)),
                dma((8,)), dma((8,)),
                dma((2, nx - 1)), dma((2, nx - 1)),
                dma((2, ny - 1)), dma((2, ny - 1)),
            ],
            compiler_params=pltpu.CompilerParams(
                collective_id=0, has_side_effects=True, vmem_limit_bytes=40 * 1024 * 1024),
        )(*args)
        return pl.pallas_call(
            combine,
            out_shape=(hbm, hbm),
            in_specs=[pl.BlockSpec(memory_space=pltpu.VMEM)] * 2,
            out_specs=[pl.BlockSpec(memory_space=pltpu.HBM)] * 2,
            scratch_shapes=[
                pltpu.VMEM((groups, height, L), f32), pltpu.VMEM((groups, height, L), f32),
                dma((2 * groups * pieces,))],
            compiler_params=pltpu.CompilerParams(vmem_limit_bytes=8 * 1024 * 1024),
        )(basis, coefs)

    in_specs = (P("gx", "gy"), P("gx", "gy"), P("gx", "gy"), P(None, "gx"), P(None, "gy"))
    out_specs = (P("gx", "gy"), P("gx", "gy"))
    return jax.shard_map(body, mesh=mesh, in_specs=in_specs, out_specs=out_specs, check_vma=False)
```

```python
import jax
import jax.numpy as jnp
from jax import lax
from jax.experimental import pallas as pl
from jax.experimental.pallas import tpu as pltpu
from jax.sharding import PartitionSpec as P

ITERS = 4
CENTER = 4.0 + 0.05
L = 128
PAD = 16
EDGE = 8
MESH = pl.DeviceIdType.MESH
PIECES = [pl.ds(0, ITERS), pl.ds(8, 1)]
SIDES = [(-1, 0), (1, 0), (0, -1), (0, 1), (-1, -1), (-1, 1), (1, -1), (1, 1)]


def solve_small(gram):
    n = ITERS

    def g(a, b):
        return gram[(min(a, b), max(a, b))]

    f = {}
    for a in range(n + 1):
        for j in range(n):
            value = CENTER * g(a, j) + 2.0 * g(a, j + 1)
            f[a, j] = value + 2.0 * g(a, j - 1) if j else value
    m = {}
    for i in range(n):
        for j in range(i + 1):
            value = CENTER * f[i, j] + 2.0 * f[i + 1, j]
            m[i, j] = value + 2.0 * f[i - 1, j] if i else value
    inv, low, scaled = [], {}, {}
    for j in range(n):
        for i in range(j, n):
            acc = m[i, j]
            for k in range(j):
                acc = acc - scaled[i, k] * low[j, k]
            scaled[i, j] = acc
        inv.append(1.0 / scaled[j, j])
        for i in range(j + 1, n):
            low[i, j] = scaled[i, j] * inv[j]
    forward = []
    for i in range(n):
        acc = f[0, i]
        for k in range(i):
            acc = acc - low[i, k] * forward[k]
        forward.append(acc)
    y = [None] * n
    for i in reversed(range(n)):
        acc = forward[i] * inv[i]
        for k in range(i + 1, n):
            acc = acc - low[k, i] * y[k]
        y[i] = acc
    res = []
    for k in range(n + 1):
        z = 0.0
        if k < n:
            z = z + CENTER * y[k]
        if k >= 1:
            z = z + 2.0 * y[k - 1]
        if k + 1 < n:
            z = z + 2.0 * y[k + 1]
        res.append(1.0 - z if k == 0 else -z)
    return y, res


def kernel(nx, ny, b_hbm, dx_hbm, dy_hbm, rows_hbm, cols_hbm, basis_all, coefs,
           ext, rows_v, cols_v, rows_t, ct_hi, ct_lo, col_out, col_in, diag_out, diag_in,
           part, got_x, sum_x, got_y, in_sem, hs_sem, hr_sem, xs_sem, xr_sem, ys_sem, yr_sem):
    gx, gy = lax.axis_index("gx"), lax.axis_index("gy")
    height, width = b_hbm.shape
    groups = width // L
    sketch_dim = rows_hbm.shape[0]
    last = groups
    block = 128
    blocks = height // block
    basis = basis_all.at[pl.ds(1, ITERS)]

    loads = []
    order = [0, groups - 1] + list(range(1, groups - 1))
    for p in order:
        for a, src in enumerate((b_hbm, dx_hbm, dy_hbm)):
            copy = pltpu.make_async_copy(
                src.at[:, pl.ds(p * L, L)], ext.at[a, p, pl.ds(PAD, height), :], in_sem.at[a * groups + p])
            copy.start()
            loads.append(copy)
    for s, (src, dst) in enumerate(((cols_hbm, cols_v), (rows_hbm, rows_v))):
        copy = pltpu.make_async_copy(src, dst, in_sem.at[3 * groups + s])
        copy.start()
        loads.append(copy)

    def device(ox, oy):
        return {"gx": lax.rem(gx + (ox + nx), nx), "gy": lax.rem(gy + (oy + ny), ny)}

    def inside(sx, sy):
        return (gx + sx >= 0) & (gx + sx < nx) & (gy + sy >= 0) & (gy + sy < ny)

    peers = [(o, 0) for o in range(1, nx)] + [(0, o) for o in range(1, ny)]
    corners = SIDES[4:]
    barrier = pltpu.get_barrier_semaphore()
    lane = lax.broadcasted_iota(jnp.int32, (EDGE, L), 1)
    tall_lane = lax.broadcasted_iota(jnp.int32, (height, L), 1)
    one, zero = jnp.float32(1.0), jnp.float32(0.0)
    has_up = jnp.where(gx > 0, one, zero)
    has_down = jnp.where(gx < nx - 1, one, zero)
    has_left = jnp.where(gy > 0, one, zero)
    has_right = jnp.where(gy < ny - 1, one, zero)
    col_mask = jnp.where(lane < L // 2, has_right, has_left)
    empty = jnp.zeros((EDGE, L), jnp.float32)
    bottom = PAD + height
    diag_in[...] = jnp.zeros_like(diag_in)
    col_in[...] = jnp.zeros_like(col_in)
    for p in range(groups):
        for a in range(3):
            ext[a, p, pl.ds(PAD - EDGE, EDGE), :] = empty
            ext[a, p, pl.ds(bottom, EDGE), :] = empty
    def greet(ox, oy):
        pl.semaphore_signal(barrier, inc=1, device_id=device(ox, oy), device_id_type=MESH)

    for ox, oy in peers:
        greet(ox, oy)
    for sx, sy in corners:
        pl.when(inside(sx, sy))(lambda sx=sx, sy=sy: greet(sx, sy))
    for p in range(groups + 1):
        for at in (0, bottom + EDGE):
            ext[0, p, pl.ds(at, EDGE), :] = empty
            for k in range(ITERS - 1):
                basis[k, p, pl.ds(at, EDGE), :] = empty
    part[...] = jnp.zeros_like(part)

    for copy in loads[:6]:
        copy.wait()
    for a in range(3):
        packed = jnp.where(
            tall_lane < L // 2, ext[a, 0, pl.ds(PAD, height), :], ext[a, groups - 1, pl.ds(PAD, height), :])
        diag_out[0, a] = packed[:EDGE]
        diag_out[1, a] = packed[height - EDGE:]
        turned = jnp.transpose(packed)
        col_out[0, a] = turned[:EDGE]
        col_out[1, a] = turned[L - EDGE:]
    greeted = len(peers)
    for sx, sy in corners:
        greeted = greeted + inside(sx, sy).astype(jnp.int32)
    pl.semaphore_wait(barrier, greeted)

    sends = []
    for d, (sx, sy) in reversed(list(enumerate(SIDES))):
        if sy == 0:
            src_at, dst_at = (PAD, bottom) if sx < 0 else (bottom - EDGE, PAD - EDGE)
            src = ext.at[:, pl.ds(0, groups), pl.ds(src_at, EDGE), :]
            dst = ext.at[:, pl.ds(0, groups), pl.ds(dst_at, EDGE), :]
        elif sx == 0:
            src, dst = col_out.at[int(sy > 0)], col_in.at[int(sy > 0)]
        else:
            src, dst = diag_out.at[int(sx > 0)], diag_in.at[d - 4]
        copy = pltpu.make_async_remote_copy(
            src_ref=src, dst_ref=dst, send_sem=hs_sem.at[d], recv_sem=hr_sem.at[d],
            device_id=device(sx, sy), device_id_type=MESH)
        if d == 1:
            for load in loads[6:3 * groups]:
                load.wait()
        pl.when(inside(sx, sy))(copy.start)
        sends.append((copy, sx, sy))
    keep = pltpu.make_async_copy(
        ext.at[0, pl.ds(0, groups), pl.ds(PAD, height), :],
        basis_all.at[0, pl.ds(0, groups), pl.ds(PAD, height), :], in_sem.at[3 * groups + 2])
    keep.start()

    for copy in loads[3 * groups:]:
        copy.wait()
    turned_cols = jnp.transpose(cols_v[...])
    high = turned_cols.astype(jnp.bfloat16)
    ct_hi[...] = high
    ct_lo[...] = (turned_cols - high.astype(jnp.float32)).astype(jnp.bfloat16)
    rows_t[...] = jnp.transpose(rows_v[...])

    def sketch_block(view, i):
        field = jnp.concatenate(
            [view[p, pl.ds(PAD + i * block, block), :] for p in range(groups)], axis=1)
        hi = field.astype(jnp.bfloat16)
        lo = (field - hi.astype(jnp.float32)).astype(jnp.bfloat16)
        dot = lambda u, v: jnp.dot(u, v, preferred_element_type=jnp.float32)
        product = dot(hi, ct_hi[...]) + dot(hi, ct_lo[...]) + dot(lo, ct_hi[...])
        product = product * rows_t[pl.ds(i * block, block), :]
        return jnp.sum(product.reshape(block // 8, 8, sketch_dim), axis=0)

    def view_of(k):
        return ext.at[0] if k == 0 else basis.at[k - 1]

    def stencil(k, at, row_mask=None):
        src, out = view_of(k - 1), view_of(k)
        mid = [src[p, pl.ds(at, EDGE), :] for p in range(groups + 1)]
        from_left = [pltpu.roll(v, 1, 1) for v in mid]
        from_right = [pltpu.roll(v, L - 1, 1) for v in mid]
        for p in range(groups + 1 if k < ITERS else groups):
            left = jnp.where(lane == 0, from_left[p - 1], from_left[p])
            right = jnp.where(lane == L - 1, from_right[(p + 1) % (groups + 1)], from_right[p])
            up = src[p, pl.ds(at - 1, EDGE), :]
            down = src[p, pl.ds(at + 1, EDGE), :]
            total = (up + down) + ext[1, p, pl.ds(at, EDGE), :] * (up - down)
            total = total + ((left + right) + ext[2, p, pl.ds(at, EDGE), :] * (left - right))
            value = -0.5 * total
            if k >= 2:
                value = value - view_of(k - 2)[p, pl.ds(at, EDGE), :]
            if p == last:
                value = value * col_mask
            if row_mask is not None:
                value = value * row_mask
            out[p, pl.ds(at, EDGE), :] = value

    def close(k, total):
        part[pl.ds(k if k < ITERS else 8, 1), :] = jnp.sum(total, axis=0, keepdims=True)

    nothing = jnp.zeros((8, sketch_dim), jnp.float32)
    close(0, lax.fori_loop(0, blocks, lambda i, t: t + sketch_block(view_of(0), i), nothing))

    for copy, sx, sy in sends:
        pl.when(inside(-sx, -sy))(copy.wait_recv)
    for copy, sx, sy in sends:
        pl.when(inside(sx, sy))(copy.wait_send)
    gap = jnp.zeros((L - 2 * EDGE, height), jnp.float32)
    for a in range(3):
        beside = jnp.transpose(jnp.concatenate([col_in[0, a], gap, col_in[1, a]], axis=0))
        ext[a, last, pl.ds(PAD, height), :] = beside
        above = jnp.where(lane < L // 2, diag_in[2, a], diag_in[3, a])
        below = jnp.where(lane < L // 2, diag_in[0, a], diag_in[1, a])
        ext[a, last, pl.ds(PAD - EDGE, EDGE), :] = above
        ext[a, last, pl.ds(bottom, EDGE), :] = below
    def start(src, got, send, recv, count, along, piece):
        copies = []
        rows = PIECES[piece]
        for o in range(1, count):
            copy = pltpu.make_async_remote_copy(
                src_ref=src.at[rows], dst_ref=got.at[o - 1, rows],
                send_sem=send.at[piece, o - 1], recv_sem=recv.at[piece, o - 1],
                device_id=device(*((o, 0) if along == 0 else (0, o))), device_id_type=MESH)
            copy.start()
            copies.append(copy)
        return copies

    def finish(copies, src, got, piece):
        rows = PIECES[piece]
        for copy in copies:
            copy.wait()
        total = src[rows]
        for o in range(len(copies)):
            total = total + got[o, rows]
        return total

    def along_x(piece):
        return start(part, got_x, xs_sem, xr_sem, nx, 0, piece)

    def along_y(piece):
        return start(sum_x, got_y, ys_sem, yr_sem, ny, 1, piece)

    for k in range(1, ITERS + 1):
        if k < ITERS:
            stencil(k, PAD - EDGE, has_up)
            stencil(k, bottom, has_down)

        def rows(i, k=k):
            for s in range(block // EDGE):
                stencil(k, PAD + i * block + s * EDGE)

        def step(i, total, k=k):
            rows(i)
            return total + sketch_block(view_of(k), i - 1)

        rows(0)
        if k >= 2:
            close(k - 1, total + sketch_block(view_of(k - 1), blocks - 1))
        if k == ITERS:
            early = along_x(0)
        total = lax.fori_loop(1, blocks, step, nothing)
    close(ITERS, total + sketch_block(view_of(ITERS), blocks - 1))

    late = along_x(1)
    sum_x[PIECES[0]] = finish(early, part, got_x, 0)
    early = along_y(0)
    sum_x[PIECES[1]] = finish(late, part, got_x, 1)
    late = along_y(1)
    sums = finish(early, sum_x, got_y, 0), finish(late, sum_x, got_y, 1)
    whole = [piece[k:k + 1] for piece in sums for k in range(piece.shape[0])]

    gram = {}
    for a in range(ITERS + 1):
        for c in range(a, ITERS + 1):
            entry = jnp.sum(whole[a] * whole[c], axis=1, keepdims=True)
            gram[a, c] = jnp.broadcast_to(entry, (EDGE, L))
    y, res = solve_small(gram)
    for k, value in enumerate(y + res):
        coefs[k] = value
    keep.wait()


def combine(basis, coefs, x_hbm, r_hbm, x_v, r_v, sem):
    groups, height = x_v.shape[0], x_v.shape[1]
    block = 128

    def rows(i, _):
        y = [coefs[k] for k in range(ITERS)]
        res = [coefs[ITERS + k] for k in range(ITERS + 1)]
        for p in range(groups):
            for s in range(4):
                at = i * 32 + s * EDGE
                v = [basis[k, p, pl.ds(PAD + at, EDGE), :] for k in range(ITERS + 1)]
                x, r = y[0] * v[0], res[0] * v[0]
                for k in range(1, ITERS + 1):
                    if k < ITERS:
                        x = x + y[k] * v[k]
                    r = r + res[k] * v[k]
                x_v[p, pl.ds(at, EDGE), :] = x
                r_v[p, pl.ds(at, EDGE), :] = r
        return 0

    stores = []
    for q in range(height // block):
        lax.fori_loop(q * (block // 32), (q + 1) * (block // 32), rows, 0)
        for o, (src, dst) in enumerate(((x_v, x_hbm), (r_v, r_hbm))):
            for p in range(groups):
                copy = pltpu.make_async_copy(
                    src.at[p, pl.ds(q * block, block), :],
                    dst.at[pl.ds(q * block, block), pl.ds(p * L, L)],
                    sem.at[(q * 2 + o) * groups + p])
                copy.start()
                stores.append(copy)
    for copy in stores:
        copy.wait()


def solution(mesh):
    nx, ny = mesh.shape["gx"], mesh.shape["gy"]

    def body(right_side, drift_x, drift_y, sketch_rows, sketch_cols):
        height, width = right_side.shape
        groups = width // L
        dim = sketch_rows.shape[0]
        tall = height + 2 * PAD
        f32, bf16 = jnp.float32, jnp.bfloat16
        dma = pltpu.SemaphoreType.DMA
        pieces = height // 128
        hbm = pltpu.HBM((height, width), f32)
        args = [pltpu.with_memory_space_constraint(v, pltpu.HBM)
                for v in (right_side, drift_x, drift_y, sketch_rows, sketch_cols)]
        basis, coefs = pl.pallas_call(
            lambda *refs: kernel(nx, ny, *refs),
            out_shape=(
                pltpu.VMEM((ITERS + 1, groups + 1, tall, L), f32), pltpu.VMEM((2 * ITERS + 1, EDGE, L), f32)),
            in_specs=[pl.BlockSpec(memory_space=pltpu.HBM)] * 5,
            out_specs=[pl.BlockSpec(memory_space=pltpu.VMEM)] * 2,
            scratch_shapes=[
                pltpu.VMEM((3, groups + 1, tall, L), f32),
                pltpu.VMEM((dim, height), f32),
                pltpu.VMEM((dim, width), f32),
                pltpu.VMEM((height, dim), f32),
                pltpu.VMEM((width, dim), bf16),
                pltpu.VMEM((width, dim), bf16),
                pltpu.VMEM((2, 3, EDGE, height), f32),
                pltpu.VMEM((2, 3, EDGE, height), f32),
                pltpu.VMEM((2, 3, EDGE, L), f32),
                pltpu.VMEM((4, 3, EDGE, L), f32),
                pltpu.VMEM((16, dim), f32),
                pltpu.VMEM((nx - 1, 16, dim), f32),
                pltpu.VMEM((16, dim), f32),
                pltpu.VMEM((ny - 1, 16, dim), f32),
                dma((3 * groups + 3,)),
                dma((8,)), dma((8,)),
                dma((2, nx - 1)), dma((2, nx - 1)),
                dma((2, ny - 1)), dma((2, ny - 1)),
            ],
            compiler_params=pltpu.CompilerParams(
                collective_id=0, has_side_effects=True, vmem_limit_bytes=40 * 1024 * 1024),
        )(*args)
        return pl.pallas_call(
            combine,
            out_shape=(hbm, hbm),
            in_specs=[pl.BlockSpec(memory_space=pltpu.VMEM)] * 2,
            out_specs=[pl.BlockSpec(memory_space=pltpu.HBM)] * 2,
            scratch_shapes=[
                pltpu.VMEM((groups, height, L), f32), pltpu.VMEM((groups, height, L), f32),
                dma((2 * groups * pieces,))],
            compiler_params=pltpu.CompilerParams(vmem_limit_bytes=8 * 1024 * 1024),
        )(basis, coefs)

    in_specs = (P("gx", "gy"), P("gx", "gy"), P("gx", "gy"), P(None, "gx"), P(None, "gy"))
    out_specs = (P("gx", "gy"), P("gx", "gy"))
    return jax.shard_map(body, mesh=mesh, in_specs=in_specs, out_specs=out_specs, check_vma=False)
```

```python
import jax
import jax.numpy as jnp
from jax import lax
from jax.experimental import pallas as pl
from jax.experimental.pallas import tpu as pltpu
from jax.sharding import PartitionSpec as P

ITERS = 4
CENTER = 4.0 + 0.05
L = 128
PAD = 16
EDGE = 8
MESH = pl.DeviceIdType.MESH
PIECES = [pl.ds(0, ITERS), pl.ds(8, 1)]
SIDES = [(-1, 0), (1, 0), (0, -1), (0, 1), (-1, -1), (-1, 1), (1, -1), (1, 1)]


def solve_small(gram):
    n = ITERS

    def g(a, b):
        return gram[(min(a, b), max(a, b))]

    f = {}
    for a in range(n + 1):
        for j in range(n):
            value = CENTER * g(a, j) + 2.0 * g(a, j + 1)
            f[a, j] = value + 2.0 * g(a, j - 1) if j else value
    m = {}
    for i in range(n):
        for j in range(i + 1):
            value = CENTER * f[i, j] + 2.0 * f[i + 1, j]
            m[i, j] = value + 2.0 * f[i - 1, j] if i else value
    inv, low, scaled = [], {}, {}
    for j in range(n):
        for i in range(j, n):
            acc = m[i, j]
            for k in range(j):
                acc = acc - scaled[i, k] * low[j, k]
            scaled[i, j] = acc
        inv.append(1.0 / scaled[j, j])
        for i in range(j + 1, n):
            low[i, j] = scaled[i, j] * inv[j]
    forward = []
    for i in range(n):
        acc = f[0, i]
        for k in range(i):
            acc = acc - low[i, k] * forward[k]
        forward.append(acc)
    y = [None] * n
    for i in reversed(range(n)):
        acc = forward[i] * inv[i]
        for k in range(i + 1, n):
            acc = acc - low[k, i] * y[k]
        y[i] = acc
    res = []
    for k in range(n + 1):
        z = 0.0
        if k < n:
            z = z + CENTER * y[k]
        if k >= 1:
            z = z + 2.0 * y[k - 1]
        if k + 1 < n:
            z = z + 2.0 * y[k + 1]
        res.append(1.0 - z if k == 0 else -z)
    return y, res


def kernel(nx, ny, b_hbm, dx_hbm, dy_hbm, rows_hbm, cols_hbm, basis_all, coefs,
           ext, rows_v, cols_v, rows_t, ct_hi, ct_lo, col_out, col_in, diag_out, diag_in,
           part, got_x, sum_x, got_y, in_sem, hs_sem, hr_sem, xs_sem, xr_sem, ys_sem, yr_sem):
    gx, gy = lax.axis_index("gx"), lax.axis_index("gy")
    height, width = b_hbm.shape
    groups = width // L
    sketch_dim = rows_hbm.shape[0]
    last = groups
    block = 128
    blocks = height // block
    basis = basis_all.at[pl.ds(1, ITERS)]

    loads = []
    order = [0, groups - 1] + list(range(1, groups - 1))
    for p in order:
        for a, src in enumerate((b_hbm, dx_hbm, dy_hbm)):
            copy = pltpu.make_async_copy(
                src.at[:, pl.ds(p * L, L)], ext.at[a, p, pl.ds(PAD, height), :], in_sem.at[a * groups + p])
            copy.start()
            loads.append(copy)
    for s, (src, dst) in enumerate(((cols_hbm, cols_v), (rows_hbm, rows_v))):
        copy = pltpu.make_async_copy(src, dst, in_sem.at[3 * groups + s])
        copy.start()
        loads.append(copy)

    def device(ox, oy):
        return {"gx": lax.rem(gx + (ox + nx), nx), "gy": lax.rem(gy + (oy + ny), ny)}

    def inside(sx, sy):
        return (gx + sx >= 0) & (gx + sx < nx) & (gy + sy >= 0) & (gy + sy < ny)

    peers = [(o, 0) for o in range(1, nx)] + [(0, o) for o in range(1, ny)]
    corners = SIDES[4:]
    barrier = pltpu.get_barrier_semaphore()
    lane = lax.broadcasted_iota(jnp.int32, (EDGE, L), 1)
    tall_lane = lax.broadcasted_iota(jnp.int32, (height, L), 1)
    one, zero = jnp.float32(1.0), jnp.float32(0.0)
    has_up = jnp.where(gx > 0, one, zero)
    has_down = jnp.where(gx < nx - 1, one, zero)
    has_left = jnp.where(gy > 0, one, zero)
    has_right = jnp.where(gy < ny - 1, one, zero)
    col_mask = jnp.where(lane < L // 2, has_right, has_left)
    empty = jnp.zeros((EDGE, L), jnp.float32)
    bottom = PAD + height
    diag_in[...] = jnp.zeros_like(diag_in)
    col_in[...] = jnp.zeros_like(col_in)
    for p in range(groups):
        for a in range(3):
            ext[a, p, pl.ds(PAD - EDGE, EDGE), :] = empty
            ext[a, p, pl.ds(bottom, EDGE), :] = empty
    def greet(ox, oy):
        pl.semaphore_signal(barrier, inc=1, device_id=device(ox, oy), device_id_type=MESH)

    for ox, oy in peers:
        greet(ox, oy)
    for sx, sy in corners:
        pl.when(inside(sx, sy))(lambda sx=sx, sy=sy: greet(sx, sy))
    for p in range(groups + 1):
        for at in (0, bottom + EDGE):
            ext[0, p, pl.ds(at, EDGE), :] = empty
            for k in range(ITERS - 1):
                basis[k, p, pl.ds(at, EDGE), :] = empty
    part[...] = jnp.zeros_like(part)

    for copy in loads[:6]:
        copy.wait()
    for a in range(3):
        packed = jnp.where(
            tall_lane < L // 2, ext[a, 0, pl.ds(PAD, height), :], ext[a, groups - 1, pl.ds(PAD, height), :])
        diag_out[0, a] = packed[:EDGE]
        diag_out[1, a] = packed[height - EDGE:]
        turned = jnp.transpose(packed)
        col_out[0, a] = turned[:EDGE]
        col_out[1, a] = turned[L - EDGE:]
    greeted = len(peers)
    for sx, sy in corners:
        greeted = greeted + inside(sx, sy).astype(jnp.int32)
    pl.semaphore_wait(barrier, greeted)

    sends = []
    for d, (sx, sy) in reversed(list(enumerate(SIDES))):
        if sy == 0:
            src_at, dst_at = (PAD, bottom) if sx < 0 else (bottom - EDGE, PAD - EDGE)
            src = ext.at[:, pl.ds(0, groups), pl.ds(src_at, EDGE), :]
            dst = ext.at[:, pl.ds(0, groups), pl.ds(dst_at, EDGE), :]
        elif sx == 0:
            src, dst = col_out.at[int(sy > 0)], col_in.at[int(sy > 0)]
        else:
            src, dst = diag_out.at[int(sx > 0)], diag_in.at[d - 4]
        copy = pltpu.make_async_remote_copy(
            src_ref=src, dst_ref=dst, send_sem=hs_sem.at[d], recv_sem=hr_sem.at[d],
            device_id=device(sx, sy), device_id_type=MESH)
        if d == 1:
            for load in loads[6:3 * groups]:
                load.wait()
        pl.when(inside(sx, sy))(copy.start)
        sends.append((copy, sx, sy))
    keep = pltpu.make_async_copy(
        ext.at[0, pl.ds(0, groups), pl.ds(PAD, height), :],
        basis_all.at[0, pl.ds(0, groups), pl.ds(PAD, height), :], in_sem.at[3 * groups + 2])
    keep.start()

    for copy in loads[3 * groups:]:
        copy.wait()
    turned_cols = jnp.transpose(cols_v[...])
    high = turned_cols.astype(jnp.bfloat16)
    ct_hi[...] = high
    ct_lo[...] = (turned_cols - high.astype(jnp.float32)).astype(jnp.bfloat16)
    rows_t[...] = jnp.transpose(rows_v[...])

    def sketch_block(view, i):
        field = jnp.concatenate(
            [view[p, pl.ds(PAD + i * block, block), :] for p in range(groups)], axis=1)
        hi = field.astype(jnp.bfloat16)
        lo = (field - hi.astype(jnp.float32)).astype(jnp.bfloat16)
        dot = lambda u, v: jnp.dot(u, v, preferred_element_type=jnp.float32)
        product = dot(hi, ct_hi[...]) + dot(hi, ct_lo[...]) + dot(lo, ct_hi[...])
        product = product * rows_t[pl.ds(i * block, block), :]
        return jnp.sum(product.reshape(block // 8, 8, sketch_dim), axis=0)

    def view_of(k):
        return ext.at[0] if k == 0 else basis.at[k - 1]

    def stencil(k, at, row_mask=None):
        src, out = view_of(k - 1), view_of(k)
        mid = [src[p, pl.ds(at, EDGE), :] for p in range(groups + 1)]
        from_left = [pltpu.roll(v, 1, 1) for v in mid]
        from_right = [pltpu.roll(v, L - 1, 1) for v in mid]
        for p in range(groups + 1 if k < ITERS else groups):
            left = jnp.where(lane == 0, from_left[p - 1], from_left[p])
            right = jnp.where(lane == L - 1, from_right[(p + 1) % (groups + 1)], from_right[p])
            up = src[p, pl.ds(at - 1, EDGE), :]
            down = src[p, pl.ds(at + 1, EDGE), :]
            total = (up + down) + ext[1, p, pl.ds(at, EDGE), :] * (up - down)
            total = total + ((left + right) + ext[2, p, pl.ds(at, EDGE), :] * (left - right))
            value = -0.5 * total
            if k >= 2:
                value = value - view_of(k - 2)[p, pl.ds(at, EDGE), :]
            if p == last:
                value = value * col_mask
            if row_mask is not None:
                value = value * row_mask
            out[p, pl.ds(at, EDGE), :] = value

    def close(k, total):
        part[pl.ds(k if k < ITERS else 8, 1), :] = jnp.sum(total, axis=0, keepdims=True)

    nothing = jnp.zeros((8, sketch_dim), jnp.float32)
    close(0, lax.fori_loop(0, blocks, lambda i, t: t + sketch_block(view_of(0), i), nothing))

    for copy, sx, sy in sends:
        pl.when(inside(-sx, -sy))(copy.wait_recv)
    for copy, sx, sy in sends:
        pl.when(inside(sx, sy))(copy.wait_send)
    gap = jnp.zeros((L - 2 * EDGE, height), jnp.float32)
    for a in range(3):
        beside = jnp.transpose(jnp.concatenate([col_in[0, a], gap, col_in[1, a]], axis=0))
        ext[a, last, pl.ds(PAD, height), :] = beside
        above = jnp.where(lane < L // 2, diag_in[2, a], diag_in[3, a])
        below = jnp.where(lane < L // 2, diag_in[0, a], diag_in[1, a])
        ext[a, last, pl.ds(PAD - EDGE, EDGE), :] = above
        ext[a, last, pl.ds(bottom, EDGE), :] = below
    def start(src, got, send, recv, count, along, piece):
        copies = []
        rows = PIECES[piece]
        for o in range(1, count):
            copy = pltpu.make_async_remote_copy(
                src_ref=src.at[rows], dst_ref=got.at[o - 1, rows],
                send_sem=send.at[piece, o - 1], recv_sem=recv.at[piece, o - 1],
                device_id=device(*((o, 0) if along == 0 else (0, o))), device_id_type=MESH)
            copy.start()
            copies.append(copy)
        return copies

    def finish(copies, src, got, piece):
        rows = PIECES[piece]
        for copy in copies:
            copy.wait()
        total = src[rows]
        for o in range(len(copies)):
            total = total + got[o, rows]
        return total

    def along_x(piece):
        return start(part, got_x, xs_sem, xr_sem, nx, 0, piece)

    def along_y(piece):
        return start(sum_x, got_y, ys_sem, yr_sem, ny, 1, piece)

    for k in range(1, ITERS + 1):
        if k < ITERS:
            stencil(k, PAD - EDGE, has_up)
            stencil(k, bottom, has_down)

        def rows(i, k=k):
            for s in range(block // EDGE):
                stencil(k, PAD + i * block + s * EDGE)

        def step(i, total, k=k):
            total = total + sketch_block(view_of(k), i - 1)
            rows(i)
            return total

        if k >= 2:
            close(k - 1, total + sketch_block(view_of(k - 1), blocks - 1))
        rows(0)
        if k == ITERS:
            early = along_x(0)
        total = lax.fori_loop(1, blocks, step, nothing)
    close(ITERS, total + sketch_block(view_of(ITERS), blocks - 1))

    late = along_x(1)
    sum_x[PIECES[0]] = finish(early, part, got_x, 0)
    early = along_y(0)
    sum_x[PIECES[1]] = finish(late, part, got_x, 1)
    late = along_y(1)
    sums = finish(early, sum_x, got_y, 0), finish(late, sum_x, got_y, 1)
    whole = [piece[k:k + 1] for piece in sums for k in range(piece.shape[0])]

    gram = {}
    for a in range(ITERS + 1):
        for c in range(a, ITERS + 1):
            entry = jnp.sum(whole[a] * whole[c], axis=1, keepdims=True)
            gram[a, c] = jnp.broadcast_to(entry, (EDGE, L))
    y, res = solve_small(gram)
    for k, value in enumerate(y + res):
        coefs[k] = value
    keep.wait()


def combine(basis, coefs, x_hbm, r_hbm, x_v, r_v, sem):
    groups, height = x_v.shape[0], x_v.shape[1]
    block = 128

    def rows(i, _):
        y = [coefs[k] for k in range(ITERS)]
        res = [coefs[ITERS + k] for k in range(ITERS + 1)]
        for p in range(groups):
            for s in range(4):
                at = i * 32 + s * EDGE
                v = [basis[k, p, pl.ds(PAD + at, EDGE), :] for k in range(ITERS + 1)]
                x, r = y[0] * v[0], res[0] * v[0]
                for k in range(1, ITERS + 1):
                    if k < ITERS:
                        x = x + y[k] * v[k]
                    r = r + res[k] * v[k]
                x_v[p, pl.ds(at, EDGE), :] = x
                r_v[p, pl.ds(at, EDGE), :] = r
        return 0

    stores = []
    for q in range(height // block):
        lax.fori_loop(q * (block // 32), (q + 1) * (block // 32), rows, 0)
        for o, (src, dst) in enumerate(((x_v, x_hbm), (r_v, r_hbm))):
            for p in range(groups):
                copy = pltpu.make_async_copy(
                    src.at[p, pl.ds(q * block, block), :],
                    dst.at[pl.ds(q * block, block), pl.ds(p * L, L)],
                    sem.at[(q * 2 + o) * groups + p])
                copy.start()
                stores.append(copy)
    for copy in stores:
        copy.wait()


def solution(mesh):
    nx, ny = mesh.shape["gx"], mesh.shape["gy"]

    def body(right_side, drift_x, drift_y, sketch_rows, sketch_cols):
        height, width = right_side.shape
        groups = width // L
        dim = sketch_rows.shape[0]
        tall = height + 2 * PAD
        f32, bf16 = jnp.float32, jnp.bfloat16
        dma = pltpu.SemaphoreType.DMA
        pieces = height // 128
        hbm = pltpu.HBM((height, width), f32)
        args = [pltpu.with_memory_space_constraint(v, pltpu.HBM)
                for v in (right_side, drift_x, drift_y, sketch_rows, sketch_cols)]
        basis, coefs = pl.pallas_call(
            lambda *refs: kernel(nx, ny, *refs),
            out_shape=(
                pltpu.VMEM((ITERS + 1, groups + 1, tall, L), f32), pltpu.VMEM((2 * ITERS + 1, EDGE, L), f32)),
            in_specs=[pl.BlockSpec(memory_space=pltpu.HBM)] * 5,
            out_specs=[pl.BlockSpec(memory_space=pltpu.VMEM)] * 2,
            scratch_shapes=[
                pltpu.VMEM((3, groups + 1, tall, L), f32),
                pltpu.VMEM((dim, height), f32),
                pltpu.VMEM((dim, width), f32),
                pltpu.VMEM((height, dim), f32),
                pltpu.VMEM((width, dim), bf16),
                pltpu.VMEM((width, dim), bf16),
                pltpu.VMEM((2, 3, EDGE, height), f32),
                pltpu.VMEM((2, 3, EDGE, height), f32),
                pltpu.VMEM((2, 3, EDGE, L), f32),
                pltpu.VMEM((4, 3, EDGE, L), f32),
                pltpu.VMEM((16, dim), f32),
                pltpu.VMEM((nx - 1, 16, dim), f32),
                pltpu.VMEM((16, dim), f32),
                pltpu.VMEM((ny - 1, 16, dim), f32),
                dma((3 * groups + 3,)),
                dma((8,)), dma((8,)),
                dma((2, nx - 1)), dma((2, nx - 1)),
                dma((2, ny - 1)), dma((2, ny - 1)),
            ],
            compiler_params=pltpu.CompilerParams(
                collective_id=0, has_side_effects=True, vmem_limit_bytes=40 * 1024 * 1024),
        )(*args)
        return pl.pallas_call(
            combine,
            out_shape=(hbm, hbm),
            in_specs=[pl.BlockSpec(memory_space=pltpu.VMEM)] * 2,
            out_specs=[pl.BlockSpec(memory_space=pltpu.HBM)] * 2,
            scratch_shapes=[
                pltpu.VMEM((groups, height, L), f32), pltpu.VMEM((groups, height, L), f32),
                dma((2 * groups * pieces,))],
            compiler_params=pltpu.CompilerParams(vmem_limit_bytes=8 * 1024 * 1024),
        )(basis, coefs)

    in_specs = (P("gx", "gy"), P("gx", "gy"), P("gx", "gy"), P(None, "gx"), P(None, "gy"))
    out_specs = (P("gx", "gy"), P("gx", "gy"))
    return jax.shard_map(body, mesh=mesh, in_specs=in_specs, out_specs=out_specs, check_vma=False)
```
